32 devices in a mesh: group: 2 (over x), seq: 16 (over z, y, core).
Axes of the slice: x: 2, y: 2, z: 4, core: 2. Of those that a mesh axis runs over, the one named last changes fastest.
Arguments:
- query_rows: bfloat16 [16384, 2048], P(('group', 'seq')), parts along dimension 0, may hold values from -5 to 5
- key_rows: bfloat16 [16384, 2048], P(('group', 'seq')), parts along dimension 0, may hold values from -5 to 5
- value_rows: bfloat16 [16384, 2048], P(('group', 'seq')), parts along dimension 0, may hold values from -5 to 5
Outputs:
- mixed_heads: bfloat16 [16384, 2048], P(('group', 'seq')), parts along dimension 0
The draws below stay inside these ranges and needn't reach their ends.
There are 2 independent parts, one for each index of `group`. The reference program is written for one: setup_inputs(seed, part) draws one part's arguments, and reference() takes and returns one part's arrays. A program takes and returns all parts, laid end to end along the dimension named above; each array names one. Nothing has to cross between parts.
All inputs are finite; a program needn't handle non-finite values.
Results may differ from the reference program's by a relative error of at most 0.0034.
Values may be sent and summed in bfloat16 or wider, within the bound.
A program may use at most 192 MiB of HBM per device.

```python
import math
import jax
import jax.numpy as jnp
from jax import lax

H = 16
DH = 128
WINDOW = 2048
BLOCK = 128
HD = 2048
TOKENS = 8192


def draw_query_rows(key, part):
    result_rows = jnp.clip(jax.random.normal(jax.random.fold_in(key, 1), (TOKENS, HD), jnp.float32), -5.0, 5.0)
    return result_rows.astype(jnp.bfloat16)


def draw_key_rows(key, part):
    result_rows = jnp.clip(jax.random.normal(jax.random.fold_in(key, 2), (TOKENS, HD), jnp.float32), -5.0, 5.0)
    return result_rows.astype(jnp.bfloat16)


def block_levels(stream_key, shape, split, low, high):
    def one(dim, shards_of):
        draws = jax.random.uniform(jax.random.fold_in(jax.random.fold_in(stream_key, 6), dim), (shards_of,), jnp.float32, low / len(split), high / len(split))
        return jnp.repeat(jnp.exp(draws), shape[dim] // shards_of).reshape((-1,) + (1,) * (len(shape) - dim - 1))

    level = one(*split[0])
    for cut in split[1:]:
        level = level * one(*cut)
    return level


def gaussian(rng, dims, width, limit, cuts=(), kind=jnp.bfloat16):
    values = jax.random.normal(rng, dims, jnp.float32) * width
    if len(cuts) > 0:
        values = block_levels(rng, dims, cuts, -0.22, 0.18) * values
    return jnp.clip(values, min=-limit, max=limit).astype(kind)


def setup_inputs(seed: int = 0, part: int = 0) -> dict:
    keys = jax.random.split(jax.random.key(seed), 4)
    part_keys = jax.random.split(jax.random.fold_in(keys[3], part), 4)
    return {
        "query_rows": draw_query_rows(jax.random.fold_in(jax.random.fold_in(keys[3], part), 71), part),
        "key_rows": draw_key_rows(jax.random.fold_in(jax.random.fold_in(keys[3], part), 71), part),
        "value_rows": gaussian(part_keys[2], (TOKENS, HD), 1.0, 5.0, ((0, 16),)),
    }


EPSILON = 1e-06

def head_norm(vectors):
    return vectors * lax.rsqrt(lax.optimization_barrier(jnp.mean(vectors * vectors, axis=-1, keepdims=True)) + EPSILON)

def linear_branch(query_rows, key_rows, value_rows):
    block_count = TOKENS // BLOCK
    q_blocks = query_rows.reshape(block_count, BLOCK, H, DH)
    k_blocks = key_rows.reshape(block_count, BLOCK, H, DH)
    v_blocks = value_rows.reshape(block_count, BLOCK, H, DH)
    causal = jnp.arange(BLOCK)[:, None] >= jnp.arange(BLOCK)[None, :]

    def advance(state_sum, pieces):
        query_block, key_block, value_block = pieces
        query_wide = query_block.astype(jnp.float32)
        key_wide = key_block.astype(jnp.float32)
        value_wide = value_block.astype(jnp.float32)
        scores = jnp.einsum('qhd,khd->hqk', query_wide, key_wide)
        scores = jnp.where(causal[None], scores, 0.0).astype(jnp.bfloat16)
        inner_term = jnp.einsum('hqk,khd->qhd', scores.astype(jnp.float32), value_wide)
        cross_term = jnp.einsum('qhd,hde->qhe', query_wide, state_sum, precision=lax.Precision.HIGHEST)
        state_sum = state_sum + jnp.einsum('khd,khe->hde', key_wide, value_wide)
        return (state_sum, cross_term + inner_term)
    start_state = jnp.zeros((H, DH, DH), jnp.float32)
    final_state, linear = lax.scan(advance, start_state, (q_blocks, k_blocks, v_blocks))
    return linear.reshape(TOKENS, H, DH)

def window_branch(query_rows, key_rows, value_rows):
    query_span = min(512, TOKENS)
    block_count = TOKENS // query_span
    padded_keys = jnp.concatenate([jnp.zeros((WINDOW, H * DH), jnp.bfloat16), key_rows], axis=0)
    padded_values = jnp.concatenate([jnp.zeros((WINDOW, H * DH), jnp.bfloat16), value_rows], axis=0)
    score_scale = 1.0 / math.sqrt(DH)

    def one_block(block_index):
        block_start = (block_index * query_span).astype(jnp.int32)
        query_block = lax.dynamic_slice_in_dim(query_rows, block_start, query_span, 0)
        query_block = query_block.reshape(query_span, H, DH).astype(jnp.float32)
        key_block = lax.dynamic_slice_in_dim(padded_keys, block_start, WINDOW + query_span, 0)
        key_block = key_block.reshape(WINDOW + query_span, H, DH).astype(jnp.float32)
        value_block = lax.dynamic_slice_in_dim(padded_values, block_start, WINDOW + query_span, 0)
        value_block = value_block.reshape(WINDOW + query_span, H, DH).astype(jnp.float32)
        query_pos = block_start + jnp.arange(query_span, dtype=jnp.int32)
        key_pos = block_start - WINDOW + jnp.arange(WINDOW + query_span, dtype=jnp.int32)
        allowed = (key_pos[None, :] <= query_pos[:, None]) & (key_pos[None, :] > query_pos[:, None] - WINDOW) & (key_pos[None, :] >= 0)
        scores = jnp.einsum('qhd,khd->hqk', query_block, key_block) * score_scale
        scores = jnp.where(allowed[None], scores, -1e+30)
        row_peak = lax.optimization_barrier(jnp.max(scores, axis=-1, keepdims=True))
        weights = jnp.exp(scores - row_peak)
        weights = weights / lax.optimization_barrier(jnp.sum(weights, axis=-1, keepdims=True))
        weights = weights.astype(jnp.bfloat16)
        return jnp.einsum('hqk,khd->qhd', weights.astype(jnp.float32), value_block)
    blocks = lax.map(one_block, jnp.arange(block_count, dtype=jnp.int32))
    return blocks.reshape(TOKENS, H, DH)

def reference(query_rows, key_rows, value_rows):
    linear = linear_branch(query_rows, key_rows, value_rows)
    window = window_branch(query_rows, key_rows, value_rows)
    mixed_out = head_norm(linear) + head_norm(window)
    return mixed_out.reshape(TOKENS, H * DH).astype(jnp.bfloat16)
```

```python
import functools
import math

import jax
import jax.numpy as jnp
from jax import lax
from jax.experimental import pallas as pl
from jax.experimental.pallas import tpu as pltpu
from jax.sharding import PartitionSpec as P

H = 16
DH = 128
WINDOW = 2048
TILE = 256
CORES = 2
LATE = 2
LAG = 2
NEXT = LAG + 1
SENT, CAME = 0, 1
AHEAD = 2
EPSILON = 1e-06
EXP_SCALE = math.log2(math.e) / math.sqrt(DH)
NEG = -1e30
F32 = jnp.float32
BF16 = jnp.bfloat16
MESH = pl.DeviceIdType.MESH


def dot_nt(a, b):
    return lax.dot_general(a, b, (((1,), (1,)), ((), ())), preferred_element_type=F32)


def dot_tn(a, b):
    return lax.dot_general(a, b, (((0,), (0,)), ((), ())), preferred_element_type=F32)


def dot_nn(a, b):
    return jnp.dot(a, b, preferred_element_type=F32)


def times_state(q, state):
    high = state.astype(BF16)
    low = (state - high.astype(F32)).astype(BF16)
    both = dot_nn(q, jnp.concatenate([high, low], axis=1))
    return both[:, :DH] + both[:, DH:]


def head_norm(x):
    return x * lax.rsqrt(jnp.mean(x * x, axis=-1, keepdims=True) + EPSILON)


def late_heads(level):
    return LATE


def kernel(
    levels, rows,
    q_hbm, k_hbm, v_hbm, out_hbm,
    qb, kb, vb, ky, vy, ob, o_part, w_part,
    o_acc, m_acc, l_acc, lin_acc, total, total_y, before, state_in, state_out, side_in, side_out,
    own_sem, m_send, m_recv, y_send, y_recv, f_send, f_recv, q_send, q_recv,
    s_send, s_recv, e_send, e_recv, b_send, b_recv, o_own, o_send, o_recv,
):
    me = lax.axis_index("seq")
    c = lax.rem(me, CORES)
    side = lax.rem(me // CORES, 2)
    level = me // (2 * CORES)
    heads = H // CORES
    first_late = heads - LATE
    span = CORES * rows
    tiles = span // TILE
    even = side == 0
    odd = side == 1
    has_before = level > 0
    has_after = level < levels - 1

    def both(*conds):
        out = conds[0]
        for x in conds[1:]:
            out = jnp.logical_and(out, x)
        return out

    def device(dz, ds, core):
        s = side if ds == 0 else 1 - side
        return {"seq": ((level + dz) * 2 + s) * CORES + core}

    mate = device(0, 0, 1 - c)

    def ahead(h):
        return both(has_after, h < heads - late_heads(level + 1))

    def here(h):
        return both(has_before, h >= heads - late_heads(level))

    def local(h):
        return both(odd, h >= first_late)

    def crossed(h):
        return jnp.logical_or(odd, jnp.logical_or(ahead(h), here(h)))

    def serves(h):
        return both(even, ahead(h))

    barrier = pltpu.get_barrier_semaphore()

    def greet(dev):
        pl.semaphore_signal(barrier, inc=1, device_id=dev, device_id_type=MESH)

    greet(mate)
    for o in range(CORES):
        greet(device(0, 1, o))

    @pl.when(has_before)
    def _():
        for o in range(CORES):
            greet(device(-1, 0, o))

    @pl.when(has_after)
    def _():
        for o in range(CORES):
            greet(device(1, 0, o))

    ends = has_before.astype(jnp.int32) + has_after.astype(jnp.int32)
    pl.semaphore_wait(barrier, 1 + CORES + CORES * ends)

    kv_hbm = (k_hbm, v_hbm)
    sources = (k_hbm, v_hbm, q_hbm)

    def columns(owner, h):
        return pl.ds(pl.multiple_of((owner * heads + h) * DH, DH), DH)

    def part(core):
        return pl.ds(pl.multiple_of(core * rows, rows), rows)

    def chip_target(t, h):
        return (kb, vb)[t].at[h, part(c), :] if t < 2 else qb.at[0, h, part(c), :]

    def own_copy(h, t):
        return pltpu.make_async_copy(
            sources[t].at[:, columns(c, h)], chip_target(t, h), own_sem.at[h, t]
        )

    def remote(src, dst, send, recv, dev):
        return pltpu.make_async_remote_copy(
            src_ref=src, dst_ref=dst, send_sem=send, recv_sem=recv,
            device_id=dev, device_id_type=MESH,
        )

    def mate_copy(h, t):
        return remote(
            sources[t].at[:, columns(1 - c, h)], chip_target(t, h),
            m_send.at[h, t], m_recv.at[h, t], mate,
        )

    def y_copy(h, o, t):
        return remote(
            kv_hbm[t].at[:, columns(o, h)], (ky, vy)[t].at[h, part(c), :],
            y_send.at[h, o, t], y_recv.at[h, c, t], device(0, 1, o),
        )

    def y_pass(h, s, t):
        b = h - first_late
        return remote(
            (kb, vb)[t].at[heads + b, part(s), :], (ky, vy)[t].at[h, part(s), :],
            y_send.at[h, s, t], y_recv.at[h, s, t], device(0, 1, c),
        )

    def f_copy(b, o, t, s):
        h = first_late + b
        return remote(
            kv_hbm[t].at[:, columns(o, h)], (kb, vb)[t].at[heads + b, part(s), :],
            f_send.at[b, o, t], f_recv.at[b, s, t], device(1, 0, o),
        )

    def q_copy(h, o, s):
        return remote(
            q_hbm.at[:, columns(o, h)], qb.at[1, h, part(s), :],
            q_send.at[h, o], q_recv.at[h, s], device(-1, 0, o),
        )

    def served_copy(h, t):
        return remote(
            (o_part, w_part)[t].at[SENT, h], (o_part, w_part)[t].at[CAME, h],
            b_send.at[h, t], b_recv.at[h, t], device(1, 0, c),
        )

    def state_copy(h):
        return remote(
            state_out.at[h], state_in.at[h], s_send.at[h], s_recv.at[h], device(1, 0, c)
        )

    def side_copy(b):
        return remote(
            side_out.at[b], side_in.at[b], e_send.at[b], e_recv.at[b], device(0, 1, c)
        )

    def out_own(h):
        return pltpu.make_async_copy(
            ob.at[h, part(c), :], out_hbm.at[:, columns(c, h)], o_own.at[h]
        )

    def out_mate(h):
        return remote(
            ob.at[h, part(1 - c), :], out_hbm.at[:, columns(c, h)],
            o_send.at[h], o_recv.at[h], mate,
        )

    def chip_start(h, t):
        own_copy(h, t).start()
        mate_copy(h, t).start()

    def chip_wait(h, t):
        own_copy(h, t).wait()
        mate_copy(h, t).wait_recv()

    def direct(h):
        return jnp.logical_or(even, ahead(h))

    def passed(h):
        return both(odd, here(h))

    def y_start(h):
        @pl.when(direct(h))
        def _():
            for t in range(2):
                for o in range(CORES):
                    y_copy(h, o, t).start()

        @pl.when(passed(h))
        def _():
            for t in range(2):
                for s in range(CORES):
                    f_copy(h - first_late, c, t, s).wait_recv()
                    y_pass(h, s, t).start()

    def y_sent(h):
        @pl.when(jnp.logical_or(direct(h), passed(h)))
        def _():
            for t in range(2):
                for o in range(CORES):
                    y_copy(h, o, t).wait_send()

    def y_arrived(h):
        for t in range(2):
            for s in range(CORES):
                y_pass(h, s, t).wait_recv()

    def q_start(h):
        @pl.when(both(has_before, jnp.logical_not(local(h))))
        def _():
            for o in range(CORES):
                q_copy(h, o, c).start()

    row_id = lax.broadcasted_iota(jnp.int32, (TILE, TILE), 0)
    col_id = lax.broadcasted_iota(jnp.int32, (TILE, TILE), 1)
    causal = row_id >= col_id
    later = col_id > row_id

    def tile(i):
        return slice(i * TILE, (i + 1) * TILE)

    def keep_part(slot, i, q, k_full, v_full, s_diag, v_diag):
        peak = jnp.max(s_diag, axis=-1, keepdims=True)
        if k_full is not None:
            s_full = dot_nt(q, k_full)
            peak = jnp.maximum(peak, jnp.max(s_full, axis=-1, keepdims=True))
        p_diag = jnp.exp2((s_diag - peak) * EXP_SCALE)
        mass = jnp.sum(p_diag, axis=-1, keepdims=True)
        acc = dot_nn(p_diag.astype(BF16), v_diag)
        if k_full is not None:
            p_full = jnp.exp2((s_full - peak) * EXP_SCALE)
            mass = mass + jnp.sum(p_full, axis=-1, keepdims=True)
            acc = acc + dot_nn(p_full.astype(BF16), v_full)
        o_acc[slot, tile(i), :] = acc
        m_acc[slot, tile(i), :] = jnp.broadcast_to(peak, (TILE, DH))
        l_acc[slot, tile(i), :] = jnp.broadcast_to(mass, (TILE, DH))

    def own_part(h, slot):
        state = jnp.zeros((DH, DH), F32)
        for i in range(tiles):
            q, k, v = qb[0, h, tile(i), :], kb[h, tile(i), :], vb[h, tile(i), :]
            scores = dot_nt(q, k)
            lin = dot_nn(jnp.where(causal, scores, 0.0).astype(BF16), v)
            if i > 0:
                lin = lin + times_state(q, state)
            lin_acc[slot, tile(i), :] = lin
            state = state + dot_tn(k, v)
            k_full = kb[h, : i * TILE, :] if i > 0 else None
            v_full = vb[h, : i * TILE, :] if i > 0 else None
            keep_part(slot, i, q, k_full, v_full, jnp.where(causal, scores, NEG), v)
        total[h] = state

    def next_part(which, h, held):
        for i in range(tiles):
            q, k, v = qb[which, h, tile(i), :], kb[held, tile(i), :], vb[held, tile(i), :]
            scores = jnp.where(later, dot_nt(q, k), NEG)
            k_full = kb[held, (i + 1) * TILE :, :] if i < tiles - 1 else None
            v_full = vb[held, (i + 1) * TILE :, :] if i < tiles - 1 else None
            keep_part(NEXT, i, q, k_full, v_full, scores, v)

    def cross_part(h, which, slot):
        for i in range(tiles):
            s = dot_nt(qb[which, h, tile(i), :], ky[h])
            old = m_acc[slot, tile(i), :]
            peak = jnp.maximum(old, jnp.max(s, axis=-1, keepdims=True))
            keep = jnp.exp2((old - peak) * EXP_SCALE)
            p = jnp.exp2((s - peak[:, :1]) * EXP_SCALE)
            l_acc[slot, tile(i), :] = l_acc[slot, tile(i), :] * keep + jnp.sum(
                p, axis=-1, keepdims=True
            )
            o_acc[slot, tile(i), :] = o_acc[slot, tile(i), :] * keep + dot_nn(
                p.astype(BF16), vy[h]
            )
            m_acc[slot, tile(i), :] = peak

    def serve(h):
        for i in range(tiles):
            mass = l_acc[NEXT, tile(i), :]
            o_part[SENT, h, tile(i), :] = (o_acc[NEXT, tile(i), :] / mass).astype(BF16)
            weight = m_acc[NEXT, tile(i), :] * EXP_SCALE + jnp.log2(mass)
            w_part[SENT, h, :, tile(i)] = weight.T[:1, :]

        @pl.when(jnp.logical_not(local(h)))
        def _():
            served_copy(h, 0).start()
            served_copy(h, 1).start()

    def merge_back(h, slot):
        @pl.when(jnp.logical_not(local(h)))
        def _():
            served_copy(h, 0).wait_recv()
            served_copy(h, 1).wait_recv()

        src = jnp.where(local(h), SENT, CAME)
        for i in range(tiles):
            weight = jnp.broadcast_to(w_part[src, h, :, tile(i)], (DH, TILE)).T
            old = m_acc[slot, tile(i), :]
            peak = jnp.maximum(old, weight * (1.0 / EXP_SCALE))
            keep = jnp.exp2((old - peak) * EXP_SCALE)
            take = jnp.exp2(weight - peak * EXP_SCALE)
            mean = o_part[src, h, tile(i), :].astype(F32)
            o_acc[slot, tile(i), :] = o_acc[slot, tile(i), :] * keep + mean * take
            l_acc[slot, tile(i), :] = l_acc[slot, tile(i), :] * keep + take
            m_acc[slot, tile(i), :] = peak

    def add_state(h, slot):
        state = before[h]
        for i in range(tiles):
            lin = lin_acc[slot, tile(i), :] + times_state(qb[0, h, tile(i), :], state)
            lin_acc[slot, tile(i), :] = head_norm(lin)

    def emit(h, slot):
        for i in range(tiles):
            win = o_acc[slot, tile(i), :] / l_acc[slot, tile(i), :]
            ob[h, tile(i), :] = (lin_acc[slot, tile(i), :] + head_norm(win)).astype(BF16)
        out_mate(h).start()
        out_own(h).start()

    def chain(h):
        @pl.when(has_before)
        def _():
            state_copy(h).wait_recv()
            before[h] = state_in[h]

        @pl.when(level == 0)
        def _():
            before[h] = jnp.zeros((DH, DH), F32)

        @pl.when(jnp.logical_or(odd, here(h)))
        def _():
            before[h] += total_y[h]

        @pl.when(has_after)
        def _():
            state_out[h] = before[h] + total[h]

            @pl.when(serves(h))
            def _():
                state_out[h] += total_y[h]

            state_copy(h).start()

    side_sends = jnp.logical_or(even, has_before)
    side_gets = jnp.logical_or(odd, has_before)

    def chain_late(b):
        h = first_late + b

        @pl.when(has_before)
        def _():
            state_copy(h).wait_recv()
            before[h] = state_in[h]

        @pl.when(level == 0)
        def _():
            before[h] = jnp.zeros((DH, DH), F32)

        @pl.when(has_after)
        def _():
            state_out[h] = before[h] + total[h]
            state_copy(h).start()

        @pl.when(even)
        def _():
            side_out[b] = before[h] + total[h]

        @pl.when(odd)
        def _():
            side_out[b] = before[h]

        @pl.when(side_sends)
        def _():
            side_copy(b).start()

    y_start(0)

    q_start(0)
    for t in range(3):
        chip_start(0, t)
    for b in range(LATE):
        for t in range(2):
            chip_start(first_late + b, t)
    for g in range(1, AHEAD):
        y_start(g)
    for b in range(LATE):
        q_start(first_late + b)
    q_start(1)
    for t in range(3):
        chip_start(1, t)
    for b in range(LATE):
        for t in range(2):
            chip_wait(first_late + b, t)
        total[first_late + b] = dot_tn(kb[first_late + b], vb[first_late + b])

    def step(h, _):
        slot = lax.rem(h, NEXT)
        is_late = h >= first_late
        chain_due = both(h >= 1, h <= first_late)

        for t in range(2):
            @pl.when(h + 2 < first_late)
            def _():
                chip_start(h + 2, t)

            @pl.when(jnp.logical_not(is_late))
            def _():
                chip_wait(h, t)

        @pl.when(h + 2 < heads)
        def _():
            chip_start(h + 2, 2)

        for t in range(2):
            @pl.when(both(odd, has_after, h < 2 * LATE, lax.rem(h, 2) == t))
            def _():
                @pl.when(jnp.logical_not(ahead(first_late + h // 2)))
                def _():
                    for o in range(CORES):
                        f_copy(h // 2, o, t, c).start()

        chip_wait(h, 2)
        own_part(h, slot)

        @pl.when(both(chain_due, level == 1))
        def _():
            chain(h - 1)

        @pl.when(h == lax.rem(level, heads))
        def _():
            for b in range(LATE):
                chain_late(b)

        extra = both(even, has_after, h < LATE)
        usual = jnp.logical_or(
            both(has_after, jnp.logical_not(is_late)), both(has_before, local(h))
        )

        def serve_next(j, _):
            g = jnp.where(j == 0, first_late + h, h)
            alone = local(g)

            @pl.when(jnp.logical_not(alone))
            def _():
                for s in range(CORES):
                    q_copy(g, c, s).wait_recv()

            next_part(
                jnp.where(alone, 0, 1), g, jnp.where(alone, heads + g - first_late, g)
            )

            @pl.when(jnp.logical_not(serves(g)))
            def _():
                serve(g)

            return 0

        lax.fori_loop(jnp.where(extra, 0, 1), jnp.where(usual, 2, 1), serve_next, 0)

        @pl.when(both(chain_due, level == 2))
        def _():
            chain(h - 1)

        @pl.when(h + 2 < first_late)
        def _():
            q_start(h + 2)

        def prepare(g, at):
            @pl.when(has_before)
            def _():
                merge_back(g, at)

            add_state(g, at)

        @pl.when(h >= LAG)
        def _():
            g = h - LAG
            at = lax.rem(g, NEXT)
            prepare(g, at)
            emit(g, at)

        @pl.when(is_late)
        def _():
            @pl.when(side_gets)
            def _():
                side_copy(h - first_late).wait_recv()
                before[h] += side_in[h - first_late]

            prepare(h, slot)

        @pl.when(both(chain_due, level > 2))
        def _():
            chain(h - 1)

        @pl.when(crossed(h))
        def _():
            y_arrived(h)

        y_sent(h)

        @pl.when(h + AHEAD < heads)
        def _():
            y_start(h + AHEAD)

        @pl.when(crossed(h))
        def _():
            ahead_now = serves(h)
            which = ahead_now.astype(jnp.int32)
            cross_part(h, which, jnp.where(ahead_now, NEXT, slot))

        @pl.when(serves(h))
        def _():
            serve(h)

        @pl.when(is_late)
        def _():
            emit(h, slot)

        @pl.when(jnp.logical_not(is_late))
        def _():
            @pl.when(crossed(h))
            def _():
                total_y[h] = dot_tn(ky[h], vy[h])

            @pl.when(level == 0)
            def _():
                chain(h)

        return 0

    lax.fori_loop(0, heads, step, 0)

    def drain(h, _):
        for t in range(3):
            mate_copy(h, t).wait_send()
        out_mate(h).wait_send()
        out_mate(h).wait_recv()
        out_own(h).wait()

        @pl.when(has_after)
        def _():
            @pl.when(jnp.logical_not(local(h)))
            def _():
                served_copy(h, 0).wait_send()
                served_copy(h, 1).wait_send()

            state_copy(h).wait_send()

        @pl.when(both(has_before, jnp.logical_not(local(h))))
        def _():
            for o in range(CORES):
                q_copy(h, o, c).wait_send()

        return 0

    lax.fori_loop(0, heads, drain, 0)

    @pl.when(side_sends)
    def _():
        for b in range(LATE):
            side_copy(b).wait_send()

    @pl.when(both(odd, has_after))
    def _():
        for b in range(LATE):
            @pl.when(jnp.logical_not(ahead(first_late + b)))
            def _():
                for t in range(2):
                    for o in range(CORES):
                        f_copy(b, o, t, c).wait_send()


def per_device(query_rows, key_rows, value_rows):
    rows = query_rows.shape[0]
    layer = WINDOW // rows
    assert layer == 2 * CORES
    levels = lax.axis_size("seq") // layer
    heads = H // CORES
    span = CORES * rows
    dma = pltpu.SemaphoreType.DMA
    wide = pltpu.VMEM((heads, span, DH), BF16)
    return pl.pallas_call(
        functools.partial(kernel, levels, rows),
        out_shape=jax.ShapeDtypeStruct(query_rows.shape, BF16),
        in_specs=[pl.BlockSpec(memory_space=pl.ANY)] * 3,
        out_specs=pl.BlockSpec(memory_space=pl.ANY),
        scratch_shapes=[pltpu.VMEM((2, heads, span, DH), BF16)]
        + [pltpu.VMEM((heads + LATE, span, DH), BF16)] * 2
        + [wide] * 3
        + [pltpu.VMEM((2, heads, span, DH), BF16)]
        + [pltpu.VMEM((2, heads, 1, span), F32)]
        + [pltpu.VMEM((NEXT + 1, span, DH), F32)] * 3
        + [pltpu.VMEM((NEXT, span, DH), F32)]
        + [pltpu.VMEM((heads, DH, DH), F32)] * 5
        + [pltpu.VMEM((LATE, DH, DH), F32)] * 2
        + [
            dma((heads, 3)),
            dma((heads, 3)),
            dma((heads, 3)),
            dma((heads, CORES, 2)),
            dma((heads, CORES, 2)),
            dma((LATE, CORES, 2)),
            dma((LATE, CORES, 2)),
            dma((heads, CORES)),
            dma((heads, CORES)),
            dma((heads,)),
            dma((heads,)),
            dma((LATE,)),
            dma((LATE,)),
            dma((heads, 2)),
            dma((heads, 2)),
            dma((heads,)),
            dma((heads,)),
            dma((heads,)),
        ],
        compiler_params=pltpu.CompilerParams(
            collective_id=0, has_side_effects=True, vmem_limit_bytes=56 * 2**20
        ),
    )(query_rows, key_rows, value_rows)


def solution(mesh):
    spec = P(("group", "seq"), None)
    return jax.shard_map(
        per_device, mesh=mesh, in_specs=(spec, spec, spec), out_specs=spec, check_vma=False
    )
```

```python
import functools
import math

import jax
import jax.numpy as jnp
from jax import lax
from jax.experimental import pallas as pl
from jax.experimental.pallas import tpu as pltpu
from jax.sharding import PartitionSpec as P

H = 16
DH = 128
WINDOW = 2048
TILE = 256
CORES = 2
LATE = 2
LAG = 2
NEXT = LAG + 1
SENT, CAME = 0, 1
AHEAD = 2
EPSILON = 1e-06
EXP_SCALE = math.log2(math.e) / math.sqrt(DH)
NEG = -1e30
F32 = jnp.float32
BF16 = jnp.bfloat16
MESH = pl.DeviceIdType.MESH


def dot_nt(a, b):
    return lax.dot_general(a, b, (((1,), (1,)), ((), ())), preferred_element_type=F32)


def dot_tn(a, b):
    return lax.dot_general(a, b, (((0,), (0,)), ((), ())), preferred_element_type=F32)


def dot_nn(a, b):
    return jnp.dot(a, b, preferred_element_type=F32)


def times_state(q, state):
    high = state.astype(BF16)
    low = (state - high.astype(F32)).astype(BF16)
    both = dot_nn(q, jnp.concatenate([high, low], axis=1))
    return both[:, :DH] + both[:, DH:]


def head_norm(x):
    return x * lax.rsqrt(jnp.mean(x * x, axis=-1, keepdims=True) + EPSILON)


def late_heads(level):
    return LATE


def kernel(
    levels, rows,
    q_hbm, k_hbm, v_hbm, out_hbm,
    qb, kb, vb, ky, vy, ob, o_part, w_part,
    o_acc, m_acc, l_acc, lin_acc, total, total_y, before, state_in, state_out, side_in, side_out,
    own_sem, m_send, m_recv, y_send, y_recv, f_send, f_recv, q_send, q_recv,
    s_send, s_recv, e_send, e_recv, b_send, b_recv, o_own, o_send, o_recv,
):
    me = lax.axis_index("seq")
    c = lax.rem(me, CORES)
    side = lax.rem(me // CORES, 2)
    level = me // (2 * CORES)
    heads = H // CORES
    first_late = heads - LATE
    span = CORES * rows
    tiles = span // TILE
    even = side == 0
    odd = side == 1
    has_before = level > 0
    has_after = level < levels - 1

    def both(*conds):
        out = conds[0]
        for x in conds[1:]:
            out = jnp.logical_and(out, x)
        return out

    def device(dz, ds, core):
        s = side if ds == 0 else 1 - side
        return {"seq": ((level + dz) * 2 + s) * CORES + core}

    mate = device(0, 0, 1 - c)

    def ahead(h):
        return both(has_after, h < heads - late_heads(level + 1))

    def here(h):
        return both(has_before, h >= heads - late_heads(level))

    def local(h):
        return both(odd, h >= first_late)

    def crossed(h):
        return jnp.logical_or(odd, jnp.logical_or(ahead(h), here(h)))

    def serves(h):
        return both(even, ahead(h))

    barrier = pltpu.get_barrier_semaphore()

    def greet(dev):
        pl.semaphore_signal(barrier, inc=1, device_id=dev, device_id_type=MESH)

    greet(mate)
    for o in range(CORES):
        greet(device(0, 1, o))

    @pl.when(has_before)
    def _():
        for o in range(CORES):
            greet(device(-1, 0, o))

    @pl.when(has_after)
    def _():
        for o in range(CORES):
            greet(device(1, 0, o))

    ends = has_before.astype(jnp.int32) + has_after.astype(jnp.int32)
    pl.semaphore_wait(barrier, 1 + CORES + CORES * ends)

    kv_hbm = (k_hbm, v_hbm)
    sources = (k_hbm, v_hbm, q_hbm)

    def columns(owner, h):
        return pl.ds(pl.multiple_of((owner * heads + h) * DH, DH), DH)

    def part(core):
        return pl.ds(pl.multiple_of(core * rows, rows), rows)

    def chip_target(t, h):
        return (kb, vb)[t].at[h, part(c), :] if t < 2 else qb.at[0, h, part(c), :]

    def own_copy(h, t):
        return pltpu.make_async_copy(
            sources[t].at[:, columns(c, h)], chip_target(t, h), own_sem.at[h, t]
        )

    def remote(src, dst, send, recv, dev):
        return pltpu.make_async_remote_copy(
            src_ref=src, dst_ref=dst, send_sem=send, recv_sem=recv,
            device_id=dev, device_id_type=MESH,
        )

    def mate_copy(h, t):
        return remote(
            sources[t].at[:, columns(1 - c, h)], chip_target(t, h),
            m_send.at[h, t], m_recv.at[h, t], mate,
        )

    def y_copy(h, o, t):
        return remote(
            kv_hbm[t].at[:, columns(o, h)], (ky, vy)[t].at[h, part(c), :],
            y_send.at[h, o, t], y_recv.at[h, c, t], device(0, 1, o),
        )

    def y_pass(h, s, t):
        b = h - first_late
        return remote(
            (kb, vb)[t].at[heads + b, part(s), :], (ky, vy)[t].at[h, part(s), :],
            y_send.at[h, s, t], y_recv.at[h, s, t], device(0, 1, c),
        )

    def f_copy(b, o, t, s):
        h = first_late + b
        return remote(
            kv_hbm[t].at[:, columns(o, h)], (kb, vb)[t].at[heads + b, part(s), :],
            f_send.at[b, o, t], f_recv.at[b, s, t], device(1, 0, o),
        )

    def q_copy(h, o, s):
        return remote(
            q_hbm.at[:, columns(o, h)], qb.at[1, h, part(s), :],
            q_send.at[h, o], q_recv.at[h, s], device(-1, 0, o),
        )

    def served_copy(h, t):
        return remote(
            (o_part, w_part)[t].at[SENT, h], (o_part, w_part)[t].at[CAME, h],
            b_send.at[h, t], b_recv.at[h, t], device(1, 0, c),
        )

    def state_copy(h):
        return remote(
            state_out.at[h], state_in.at[h], s_send.at[h], s_recv.at[h], device(1, 0, c)
        )

    def side_copy(b):
        return remote(
            side_out.at[b], side_in.at[b], e_send.at[b], e_recv.at[b], device(0, 1, c)
        )

    def out_own(h):
        return pltpu.make_async_copy(
            ob.at[h, part(c), :], out_hbm.at[:, columns(c, h)], o_own.at[h]
        )

    def out_mate(h):
        return remote(
            ob.at[h, part(1 - c), :], out_hbm.at[:, columns(c, h)],
            o_send.at[h], o_recv.at[h], mate,
        )

    def chip_start(h, t):
        own_copy(h, t).start()
        mate_copy(h, t).start()

    def chip_wait(h, t):
        own_copy(h, t).wait()
        mate_copy(h, t).wait_recv()

    def direct(h):
        return jnp.logical_or(even, ahead(h))

    def passed(h):
        return both(odd, here(h))

    def y_start(h):
        @pl.when(direct(h))
        def _():
            for t in range(2):
                for o in range(CORES):
                    y_copy(h, o, t).start()

        @pl.when(passed(h))
        def _():
            for t in range(2):
                for s in range(CORES):
                    f_copy(h - first_late, c, t, s).wait_recv()
                    y_pass(h, s, t).start()

    def y_sent(h):
        @pl.when(jnp.logical_or(direct(h), passed(h)))
        def _():
            for t in range(2):
                for o in range(CORES):
                    y_copy(h, o, t).wait_send()

    def y_arrived(h):
        for t in range(2):
            for s in range(CORES):
                y_pass(h, s, t).wait_recv()

    def q_start(h):
        @pl.when(both(has_before, jnp.logical_not(local(h))))
        def _():
            for o in range(CORES):
                q_copy(h, o, c).start()

    row_id = lax.broadcasted_iota(jnp.int32, (TILE, TILE), 0)
    col_id = lax.broadcasted_iota(jnp.int32, (TILE, TILE), 1)
    causal = row_id >= col_id
    later = col_id > row_id

    def tile(i):
        return slice(i * TILE, (i + 1) * TILE)

    def keep_part(slot, i, q, k_full, v_full, s_diag, v_diag):
        peak = jnp.max(s_diag, axis=-1, keepdims=True)
        if k_full is not None:
            s_full = dot_nt(q, k_full)
            peak = jnp.maximum(peak, jnp.max(s_full, axis=-1, keepdims=True))
        p_diag = jnp.exp2((s_diag - peak) * EXP_SCALE)
        mass = jnp.sum(p_diag, axis=-1, keepdims=True)
        acc = dot_nn(p_diag.astype(BF16), v_diag)
        if k_full is not None:
            p_full = jnp.exp2((s_full - peak) * EXP_SCALE)
            mass = mass + jnp.sum(p_full, axis=-1, keepdims=True)
            acc = acc + dot_nn(p_full.astype(BF16), v_full)
        o_acc[slot, tile(i), :] = acc
        m_acc[slot, tile(i), :] = jnp.broadcast_to(peak, (TILE, DH))
        l_acc[slot, tile(i), :] = jnp.broadcast_to(mass, (TILE, DH))

    def own_part(h, slot):
        state = jnp.zeros((DH, DH), F32)
        for i in range(tiles):
            q, k, v = qb[0, h, tile(i), :], kb[h, tile(i), :], vb[h, tile(i), :]
            scores = dot_nt(q, k)
            lin = dot_nn(jnp.where(causal, scores, 0.0).astype(BF16), v)
            if i > 0:
                lin = lin + times_state(q, state)
            lin_acc[slot, tile(i), :] = lin
            state = state + dot_tn(k, v)
            k_full = kb[h, : i * TILE, :] if i > 0 else None
            v_full = vb[h, : i * TILE, :] if i > 0 else None
            keep_part(slot, i, q, k_full, v_full, jnp.where(causal, scores, NEG), v)
        total[h] = state

    def next_part(which, h, held):
        for i in range(tiles):
            q, k, v = qb[which, h, tile(i), :], kb[held, tile(i), :], vb[held, tile(i), :]
            scores = jnp.where(later, dot_nt(q, k), NEG)
            k_full = kb[held, (i + 1) * TILE :, :] if i < tiles - 1 else None
            v_full = vb[held, (i + 1) * TILE :, :] if i < tiles - 1 else None
            keep_part(NEXT, i, q, k_full, v_full, scores, v)

    def cross_part(h, which, slot):
        for i in range(tiles):
            s = dot_nt(qb[which, h, tile(i), :], ky[h])
            old = m_acc[slot, tile(i), :]
            peak = jnp.maximum(old, jnp.max(s, axis=-1, keepdims=True))
            keep = jnp.exp2((old - peak) * EXP_SCALE)
            p = jnp.exp2((s - peak[:, :1]) * EXP_SCALE)
            l_acc[slot, tile(i), :] = l_acc[slot, tile(i), :] * keep + jnp.sum(
                p, axis=-1, keepdims=True
            )
            o_acc[slot, tile(i), :] = o_acc[slot, tile(i), :] * keep + dot_nn(
                p.astype(BF16), vy[h]
            )
            m_acc[slot, tile(i), :] = peak

    def serve(h):
        for i in range(tiles):
            mass = l_acc[NEXT, tile(i), :]
            o_part[SENT, h, tile(i), :] = (o_acc[NEXT, tile(i), :] / mass).astype(BF16)
            weight = m_acc[NEXT, tile(i), :] * EXP_SCALE + jnp.log2(mass)
            w_part[SENT, h, :, tile(i)] = weight.T[:1, :]

        @pl.when(jnp.logical_not(local(h)))
        def _():
            served_copy(h, 0).start()
            served_copy(h, 1).start()

    def merge_back(h, slot):
        @pl.when(jnp.logical_not(local(h)))
        def _():
            served_copy(h, 0).wait_recv()
            served_copy(h, 1).wait_recv()

        src = jnp.where(local(h), SENT, CAME)
        for i in range(tiles):
            weight = jnp.broadcast_to(w_part[src, h, :, tile(i)], (DH, TILE)).T
            old = m_acc[slot, tile(i), :]
            peak = jnp.maximum(old, weight * (1.0 / EXP_SCALE))
            keep = jnp.exp2((old - peak) * EXP_SCALE)
            take = jnp.exp2(weight - peak * EXP_SCALE)
            mean = o_part[src, h, tile(i), :].astype(F32)
            o_acc[slot, tile(i), :] = o_acc[slot, tile(i), :] * keep + mean * take
            l_acc[slot, tile(i), :] = l_acc[slot, tile(i), :] * keep + take
            m_acc[slot, tile(i), :] = peak

    def add_state(h, slot):
        state = before[h]
        for i in range(tiles):
            lin = lin_acc[slot, tile(i), :] + times_state(qb[0, h, tile(i), :], state)
            lin_acc[slot, tile(i), :] = head_norm(lin)

    def emit(h, slot):
        for i in range(tiles):
            win = o_acc[slot, tile(i), :] / l_acc[slot, tile(i), :]
            ob[h, tile(i), :] = (lin_acc[slot, tile(i), :] + head_norm(win)).astype(BF16)
        out_mate(h).start()
        out_own(h).start()

    def chain(h):
        @pl.when(has_before)
        def _():
            state_copy(h).wait_recv()
            before[h] = state_in[h]

        @pl.when(level == 0)
        def _():
            before[h] = jnp.zeros((DH, DH), F32)

        @pl.when(jnp.logical_or(odd, here(h)))
        def _():
            before[h] += total_y[h]

        @pl.when(has_after)
        def _():
            state_out[h] = before[h] + total[h]

            @pl.when(serves(h))
            def _():
                state_out[h] += total_y[h]

            state_copy(h).start()

    side_sends = jnp.logical_or(even, has_before)
    side_gets = jnp.logical_or(odd, has_before)

    def chain_late(b):
        h = first_late + b

        @pl.when(has_before)
        def _():
            state_copy(h).wait_recv()
            before[h] = state_in[h]

        @pl.when(level == 0)
        def _():
            before[h] = jnp.zeros((DH, DH), F32)

        @pl.when(has_after)
        def _():
            state_out[h] = before[h] + total[h]
            state_copy(h).start()

        @pl.when(even)
        def _():
            side_out[b] = before[h] + total[h]

        @pl.when(odd)
        def _():
            side_out[b] = before[h]

        @pl.when(side_sends)
        def _():
            side_copy(b).start()

    y_start(0)

    q_start(0)
    for t in range(3):
        chip_start(0, t)
    for b in range(LATE):
        for t in range(2):
            chip_start(first_late + b, t)
    for g in range(1, AHEAD):
        y_start(g)
    for b in range(LATE):
        q_start(first_late + b)
    q_start(1)
    for t in range(3):
        chip_start(1, t)
    for b in range(LATE):
        for t in range(2):
            chip_wait(first_late + b, t)
        total[first_late + b] = dot_tn(kb[first_late + b], vb[first_late + b])

    def step(h, _):
        slot = lax.rem(h, NEXT)
        is_late = h >= first_late
        chain_due = both(h >= 1, h <= first_late)

        for t in range(2):
            @pl.when(h + 2 < first_late)
            def _():
                chip_start(h + 2, t)

            @pl.when(jnp.logical_not(is_late))
            def _():
                chip_wait(h, t)

        @pl.when(h + 2 < heads)
        def _():
            chip_start(h + 2, 2)

        for t in range(2):
            @pl.when(both(odd, has_after, h < 2 * LATE, lax.rem(h, 2) == t))
            def _():
                @pl.when(jnp.logical_not(ahead(first_late + h // 2)))
                def _():
                    for o in range(CORES):
                        f_copy(h // 2, o, t, c).start()

        chip_wait(h, 2)
        own_part(h, slot)

        @pl.when(both(chain_due, level == 2))
        def _():
            chain(h - 1)

        @pl.when(h == lax.rem(level, heads))
        def _():
            for b in range(LATE):
                chain_late(b)

        extra = both(even, has_after, h < LATE)
        usual = jnp.logical_or(
            both(has_after, jnp.logical_not(is_late)), both(has_before, local(h))
        )

        def serve_next(j, _):
            g = jnp.where(j == 0, first_late + h, h)
            alone = local(g)

            @pl.when(jnp.logical_not(alone))
            def _():
                for s in range(CORES):
                    q_copy(g, c, s).wait_recv()

            next_part(
                jnp.where(alone, 0, 1), g, jnp.where(alone, heads + g - first_late, g)
            )

            @pl.when(jnp.logical_not(serves(g)))
            def _():
                serve(g)

            return 0

        lax.fori_loop(jnp.where(extra, 0, 1), jnp.where(usual, 2, 1), serve_next, 0)

        @pl.when(both(chain_due, level > 2))
        def _():
            chain(h - 1)

        @pl.when(h + 2 < first_late)
        def _():
            q_start(h + 2)

        def prepare(g, at):
            @pl.when(has_before)
            def _():
                merge_back(g, at)

            add_state(g, at)

        @pl.when(h >= LAG)
        def _():
            g = h - LAG
            at = lax.rem(g, NEXT)
            prepare(g, at)
            emit(g, at)

        @pl.when(is_late)
        def _():
            @pl.when(side_gets)
            def _():
                side_copy(h - first_late).wait_recv()
                before[h] += side_in[h - first_late]

            prepare(h, slot)

        @pl.when(crossed(h))
        def _():
            y_arrived(h)

        y_sent(h)

        @pl.when(h + AHEAD < heads)
        def _():
            y_start(h + AHEAD)

        @pl.when(both(crossed(h), jnp.logical_not(is_late)))
        def _():
            total_y[h] = dot_tn(ky[h], vy[h])

        @pl.when(both(level == 0, jnp.logical_not(is_late)))
        def _():
            chain(h)

        @pl.when(crossed(h))
        def _():
            ahead_now = serves(h)
            which = ahead_now.astype(jnp.int32)
            cross_part(h, which, jnp.where(ahead_now, NEXT, slot))

        @pl.when(both(level == 1, jnp.logical_not(is_late)))
        def _():
            chain(h)

        @pl.when(serves(h))
        def _():
            serve(h)

        @pl.when(is_late)
        def _():
            emit(h, slot)

        return 0

    lax.fori_loop(0, heads, step, 0)

    def drain(h, _):
        for t in range(3):
            mate_copy(h, t).wait_send()
        out_mate(h).wait_send()
        out_mate(h).wait_recv()
        out_own(h).wait()

        @pl.when(has_after)
        def _():
            @pl.when(jnp.logical_not(local(h)))
            def _():
                served_copy(h, 0).wait_send()
                served_copy(h, 1).wait_send()

            state_copy(h).wait_send()

        @pl.when(both(has_before, jnp.logical_not(local(h))))
        def _():
            for o in range(CORES):
                q_copy(h, o, c).wait_send()

        return 0

    lax.fori_loop(0, heads, drain, 0)

    @pl.when(side_sends)
    def _():
        for b in range(LATE):
            side_copy(b).wait_send()

    @pl.when(both(odd, has_after))
    def _():
        for b in range(LATE):
            @pl.when(jnp.logical_not(ahead(first_late + b)))
            def _():
                for t in range(2):
                    for o in range(CORES):
                        f_copy(b, o, t, c).wait_send()


def per_device(query_rows, key_rows, value_rows):
    rows = query_rows.shape[0]
    layer = WINDOW // rows
    assert layer == 2 * CORES
    levels = lax.axis_size("seq") // layer
    heads = H // CORES
    span = CORES * rows
    dma = pltpu.SemaphoreType.DMA
    wide = pltpu.VMEM((heads, span, DH), BF16)
    return pl.pallas_call(
        functools.partial(kernel, levels, rows),
        out_shape=jax.ShapeDtypeStruct(query_rows.shape, BF16),
        in_specs=[pl.BlockSpec(memory_space=pl.ANY)] * 3,
        out_specs=pl.BlockSpec(memory_space=pl.ANY),
        scratch_shapes=[pltpu.VMEM((2, heads, span, DH), BF16)]
        + [pltpu.VMEM((heads + LATE, span, DH), BF16)] * 2
        + [wide] * 3
        + [pltpu.VMEM((2, heads, span, DH), BF16)]
        + [pltpu.VMEM((2, heads, 1, span), F32)]
        + [pltpu.VMEM((NEXT + 1, span, DH), F32)] * 3
        + [pltpu.VMEM((NEXT, span, DH), F32)]
        + [pltpu.VMEM((heads, DH, DH), F32)] * 5
        + [pltpu.VMEM((LATE, DH, DH), F32)] * 2
        + [
            dma((heads, 3)),
            dma((heads, 3)),
            dma((heads, 3)),
            dma((heads, CORES, 2)),
            dma((heads, CORES, 2)),
            dma((LATE, CORES, 2)),
            dma((LATE, CORES, 2)),
            dma((heads, CORES)),
            dma((heads, CORES)),
            dma((heads,)),
            dma((heads,)),
            dma((LATE,)),
            dma((LATE,)),
            dma((heads, 2)),
            dma((heads, 2)),
            dma((heads,)),
            dma((heads,)),
            dma((heads,)),
        ],
        compiler_params=pltpu.CompilerParams(
            collective_id=0, has_side_effects=True, vmem_limit_bytes=56 * 2**20
        ),
    )(query_rows, key_rows, value_rows)


def solution(mesh):
    spec = P(("group", "seq"), None)
    return jax.shard_map(
        per_device, mesh=mesh, in_specs=(spec, spec, spec), out_specs=spec, check_vma=False
    )
```

```python
import functools
import math

import jax
import jax.numpy as jnp
from jax import lax
from jax.experimental import pallas as pl
from jax.experimental.pallas import tpu as pltpu
from jax.sharding import PartitionSpec as P

H = 16
DH = 128
WINDOW = 2048
TILE = 256
CORES = 2
LATE = 3
EARLY = 2
SWAP = 4
SWAP_STEP = 2
SEND_AT = (-1, -1, -1, -1, -1, -1)
LAG = 2
NEXT = LAG + 1
EXTRA = NEXT + 1
SENT, CAME = 0, 1
AHEAD = 3
EPSILON = 1e-06
EXP_SCALE = math.log2(math.e) / math.sqrt(DH)
NEG = -1e30
F32 = jnp.float32
BF16 = jnp.bfloat16
MESH = pl.DeviceIdType.MESH


def dot_nt(a, b):
    return lax.dot_general(a, b, (((1,), (1,)), ((), ())), preferred_element_type=F32)


def dot_tn(a, b):
    return lax.dot_general(a, b, (((0,), (0,)), ((), ())), preferred_element_type=F32)


def dot_nn(a, b):
    return jnp.dot(a, b, preferred_element_type=F32)


def times_state(q, state):
    high = state.astype(BF16)
    low = (state - high.astype(F32)).astype(BF16)
    both = dot_nn(q, jnp.concatenate([high, low], axis=1))
    return both[:, :DH] + both[:, DH:]


def head_norm(x):
    return x * lax.rsqrt(jnp.mean(x * x, axis=-1, keepdims=True) + EPSILON)


def late_heads(level):
    return jnp.minimum(level, LATE)


def kernel(
    levels, rows,
    q_hbm, k_hbm, v_hbm, out_hbm,
    qb, kb, vb, ob, o_part, w_part,
    o_acc, m_acc, l_acc, lin_acc, total, total_y, before, state_in, state_out, side_in, side_out,
    own_sem, m_send, m_recv, y_send, y_recv, f_send, f_recv, q_send, q_recv,
    s_send, s_recv, e_send, e_recv, b_send, b_recv, o_own, o_send, o_recv, x_send, x_recv, g_send, g_recv,
):
    me = lax.axis_index("seq")
    c = lax.rem(me, CORES)
    side = lax.rem(me // CORES, 2)
    level = me // (2 * CORES)
    heads = H // CORES
    first_late = heads - LATE
    first_early = heads - EARLY
    span = CORES * rows
    tiles = span // TILE
    even = side == 0
    odd = side == 1
    has_before = level > 0
    has_after = level < levels - 1

    def both(*conds):
        out = conds[0]
        for x in conds[1:]:
            out = jnp.logical_and(out, x)
        return out

    def device(dz, ds, core):
        s = side if ds == 0 else 1 - side
        return {"seq": ((level + dz) * 2 + s) * CORES + core}

    mate = device(0, 0, 1 - c)

    def ahead(h):
        return both(has_after, h < heads - late_heads(level + 1))

    def here(h):
        return both(has_before, h >= heads - late_heads(level))

    def local(h):
        return both(odd, here(h))

    def gives(h):
        return both(has_after, jnp.logical_or(even, ahead(h)))

    def takes(h):
        return both(has_before, jnp.logical_not(local(h)))

    def crossed(h):
        return jnp.logical_or(
            both(odd, h != SWAP), both(even, jnp.logical_or(ahead(h), here(h)))
        )

    def serves(h):
        return both(even, ahead(h))

    barrier = pltpu.get_barrier_semaphore()

    def greet(dev):
        pl.semaphore_signal(barrier, inc=1, device_id=dev, device_id_type=MESH)

    greet(mate)
    for o in range(CORES):
        greet(device(0, 1, o))

    @pl.when(has_before)
    def _():
        for o in range(CORES):
            greet(device(-1, 0, o))

    @pl.when(has_after)
    def _():
        for o in range(CORES):
            greet(device(1, 0, o))

    ends = has_before.astype(jnp.int32) + has_after.astype(jnp.int32)
    pl.semaphore_wait(barrier, 1 + CORES + CORES * ends)

    kv_hbm = (k_hbm, v_hbm)
    sources = (k_hbm, v_hbm, q_hbm)

    def columns(owner, h):
        return pl.ds(pl.multiple_of((owner * heads + h) * DH, DH), DH)

    def part(core):
        return pl.ds(pl.multiple_of(core * rows, rows), rows)

    def chip_target(t, h):
        return (kb, vb)[t].at[h, part(c), :] if t < 2 else qb.at[0, h, part(c), :]

    def own_copy(h, t):
        return pltpu.make_async_copy(
            sources[t].at[:, columns(c, h)], chip_target(t, h), own_sem.at[h, t]
        )

    def remote(src, dst, send, recv, dev):
        return pltpu.make_async_remote_copy(
            src_ref=src, dst_ref=dst, send_sem=send, recv_sem=recv,
            device_id=dev, device_id_type=MESH,
        )

    def mate_copy(h, t):
        return remote(
            sources[t].at[:, columns(1 - c, h)], chip_target(t, h),
            m_send.at[h, t], m_recv.at[h, t], mate,
        )

    def y_copy(h, o, t):
        return remote(
            kv_hbm[t].at[:, columns(o, h)], (kb, vb)[t].at[heads + h, part(c), :],
            y_send.at[h, o, t], y_recv.at[h, c, t], device(0, 1, o),
        )

    def y_pass(h, s, t):
        b = h - first_late
        return remote(
            (kb, vb)[t].at[2 * heads + b, part(s), :], (kb, vb)[t].at[heads + h, part(s), :],
            y_send.at[h, s, t], y_recv.at[h, s, t], device(0, 1, c),
        )

    def f_copy(b, o, t, s):
        h = first_late + b
        return remote(
            kv_hbm[t].at[:, columns(o, h)], (kb, vb)[t].at[2 * heads + b, part(s), :],
            f_send.at[b, o, t], f_recv.at[b, s, t], device(1, 0, o),
        )

    def q_copy(h, o, s):
        return remote(
            q_hbm.at[:, columns(o, h)], qb.at[1, h, part(s), :],
            q_send.at[h, o], q_recv.at[h, s], device(-1, 0, o),
        )

    def served_copy(h, t):
        return remote(
            (o_part, w_part)[t].at[SENT, h], (o_part, w_part)[t].at[CAME, h],
            b_send.at[h, t], b_recv.at[h, t], device(1, 0, c),
        )

    def state_copy(h):
        return remote(
            state_out.at[h], state_in.at[h], s_send.at[h], s_recv.at[h], device(1, 0, c)
        )

    def swap_query(o, s):
        return remote(
            q_hbm.at[:, columns(o, SWAP)], qb.at[0, heads, part(s), :],
            x_send.at[o], x_recv.at[s], device(0, 1, o),
        )

    def swap_copy(t):
        return remote(
            (o_part, w_part)[t].at[SENT, heads], (o_part, w_part)[t].at[CAME, heads],
            g_send.at[t], g_recv.at[t], device(0, 1, c),
        )

    def side_copy(b):
        return remote(
            side_out.at[b], side_in.at[b], e_send.at[b], e_recv.at[b], device(0, 1, c)
        )

    def out_own(h):
        return pltpu.make_async_copy(
            ob.at[h, part(c), :], out_hbm.at[:, columns(c, h)], o_own.at[h]
        )

    def out_mate(h):
        return remote(
            ob.at[h, part(1 - c), :], out_hbm.at[:, columns(c, h)],
            o_send.at[h], o_recv.at[h], mate,
        )

    def chip_start(h, t):
        own_copy(h, t).start()
        mate_copy(h, t).start()

    def chip_wait(h, t):
        own_copy(h, t).wait()
        mate_copy(h, t).wait_recv()

    def direct(h):
        return jnp.logical_or(both(even, h != SWAP), both(odd, ahead(h)))

    def y_start(h):
        @pl.when(direct(h))
        def _():
            for t in range(2):
                for o in range(CORES):
                    y_copy(h, o, t).start()

    def y_sent(h):
        @pl.when(direct(h))
        def _():
            for t in range(2):
                for o in range(CORES):
                    y_copy(h, o, t).wait_send()

    def pass_late(step):
        for b in range(LATE):
            h = first_late + b
            at = h - 3

            @pl.when(both(odd, here(h), step == at))
            def _():
                for t in range(2):
                    for s in range(CORES):
                        f_copy(b, c, t, s).wait_recv()
                        y_pass(h, s, t).start()

    def y_arrived(h):
        for t in range(2):
            for s in range(CORES):
                y_pass(h, s, t).wait_recv()

    def q_start(h):
        @pl.when(takes(h))
        def _():
            for o in range(CORES):
                q_copy(h, o, c).start()

    def send_late(step):
        count = late_heads(level + 1)
        for chunk, at in enumerate(SEND_AT):
            @pl.when(both(odd, has_after, chunk < 2 * count, step == at))
            def _():
                for o in range(CORES):
                    f_copy(LATE - count + chunk // 2, o, chunk % 2, c).start()

    row_id = lax.broadcasted_iota(jnp.int32, (TILE, TILE), 0)
    col_id = lax.broadcasted_iota(jnp.int32, (TILE, TILE), 1)
    causal = row_id >= col_id
    later = col_id > row_id

    def tile(i):
        return slice(i * TILE, (i + 1) * TILE)

    def keep_part(slot, i, q, k_full, v_full, s_diag, v_diag):
        peak = jnp.max(s_diag, axis=-1, keepdims=True)
        if k_full is not None:
            s_full = dot_nt(q, k_full)
            peak = jnp.maximum(peak, jnp.max(s_full, axis=-1, keepdims=True))
        p_diag = jnp.exp2((s_diag - peak) * EXP_SCALE)
        mass = jnp.sum(p_diag, axis=-1, keepdims=True)
        acc = dot_nn(p_diag.astype(BF16), v_diag)
        if k_full is not None:
            p_full = jnp.exp2((s_full - peak) * EXP_SCALE)
            mass = mass + jnp.sum(p_full, axis=-1, keepdims=True)
            acc = acc + dot_nn(p_full.astype(BF16), v_full)
        o_acc[slot, tile(i), :] = acc
        m_acc[slot, tile(i), :] = jnp.broadcast_to(peak, (TILE, DH))
        l_acc[slot, tile(i), :] = jnp.broadcast_to(mass, (TILE, DH))

    def own_part(h, slot):
        state = jnp.zeros((DH, DH), F32)
        for i in range(tiles):
            q, k, v = qb[0, h, tile(i), :], kb[h, tile(i), :], vb[h, tile(i), :]
            scores = dot_nt(q, k)
            lin = dot_nn(jnp.where(causal, scores, 0.0).astype(BF16), v)
            if i > 0:
                lin = lin + times_state(q, state)
            lin_acc[slot, tile(i), :] = lin
            state = state + dot_tn(k, v)
            k_full = kb[h, : i * TILE, :] if i > 0 else None
            v_full = vb[h, : i * TILE, :] if i > 0 else None
            keep_part(slot, i, q, k_full, v_full, jnp.where(causal, scores, NEG), v)
        total[h] = state

    def next_part(which, h, held):
        for i in range(tiles):
            q, k, v = qb[which, h, tile(i), :], kb[held, tile(i), :], vb[held, tile(i), :]
            scores = jnp.where(later, dot_nt(q, k), NEG)
            k_full = kb[held, (i + 1) * TILE :, :] if i < tiles - 1 else None
            v_full = vb[held, (i + 1) * TILE :, :] if i < tiles - 1 else None
            keep_part(NEXT, i, q, k_full, v_full, scores, v)

    def cross_part(which, h, held, slot):
        for i in range(tiles):
            s = dot_nt(qb[which, h, tile(i), :], kb[held])
            old = m_acc[slot, tile(i), :]
            peak = jnp.maximum(old, jnp.max(s, axis=-1, keepdims=True))
            keep = jnp.exp2((old - peak) * EXP_SCALE)
            p = jnp.exp2((s - peak[:, :1]) * EXP_SCALE)
            l_acc[slot, tile(i), :] = l_acc[slot, tile(i), :] * keep + jnp.sum(
                p, axis=-1, keepdims=True
            )
            o_acc[slot, tile(i), :] = o_acc[slot, tile(i), :] * keep + dot_nn(
                p.astype(BF16), vb[held]
            )
            m_acc[slot, tile(i), :] = peak

    def pack(slot, to):
        for i in range(tiles):
            mass = l_acc[slot, tile(i), :]
            o_part[SENT, to, tile(i), :] = (o_acc[slot, tile(i), :] / mass).astype(BF16)
            weight = m_acc[slot, tile(i), :] * EXP_SCALE + jnp.log2(mass)
            w_part[SENT, to, :, tile(i)] = weight.T[:1, :]

    def serve(h):
        pack(NEXT, h)

        @pl.when(gives(h))
        def _():
            served_copy(h, 0).start()
            served_copy(h, 1).start()

    def merge_back(h, slot):
        @pl.when(takes(h))
        def _():
            served_copy(h, 0).wait_recv()
            served_copy(h, 1).wait_recv()

        merge(jnp.where(local(h), SENT, CAME), h, slot)

    def merge(src, h, slot):
        for i in range(tiles):
            weight = jnp.broadcast_to(w_part[src, h, :, tile(i)], (DH, TILE)).T
            old = m_acc[slot, tile(i), :]
            peak = jnp.maximum(old, weight * (1.0 / EXP_SCALE))
            keep = jnp.exp2((old - peak) * EXP_SCALE)
            take = jnp.exp2(weight - peak * EXP_SCALE)
            mean = o_part[src, h, tile(i), :].astype(F32)
            o_acc[slot, tile(i), :] = o_acc[slot, tile(i), :] * keep + mean * take
            l_acc[slot, tile(i), :] = l_acc[slot, tile(i), :] * keep + take
            m_acc[slot, tile(i), :] = peak

    def add_state(h, slot):
        state = before[h]
        for i in range(tiles):
            lin = lin_acc[slot, tile(i), :] + times_state(qb[0, h, tile(i), :], state)
            lin_acc[slot, tile(i), :] = head_norm(lin)

    def emit(h, slot):
        for i in range(tiles):
            win = o_acc[slot, tile(i), :] / l_acc[slot, tile(i), :]
            ob[h, tile(i), :] = (lin_acc[slot, tile(i), :] + head_norm(win)).astype(BF16)
        out_mate(h).start()
        out_own(h).start()

    def chain(h):
        @pl.when(has_before)
        def _():
            state_copy(h).wait_recv()
            before[h] = state_in[h]

        @pl.when(level == 0)
        def _():
            before[h] = jnp.zeros((DH, DH), F32)

        @pl.when(both(odd, h == SWAP))
        def _():
            side_copy(EARLY).wait_recv()
            total_y[h] = side_in[EARLY]

        @pl.when(jnp.logical_or(odd, here(h)))
        def _():
            before[h] += total_y[h]

        @pl.when(has_after)
        def _():
            state_out[h] = before[h] + total[h]

            @pl.when(serves(h))
            def _():
                state_out[h] += total_y[h]

            state_copy(h).start()

    side_sends = jnp.logical_or(even, has_before)
    side_gets = jnp.logical_or(odd, has_before)

    def chain_early(b):
        h = first_early + b

        @pl.when(has_before)
        def _():
            state_copy(h).wait_recv()
            before[h] = state_in[h]

        @pl.when(level == 0)
        def _():
            before[h] = jnp.zeros((DH, DH), F32)

        @pl.when(has_after)
        def _():
            state_out[h] = before[h] + total[h]
            state_copy(h).start()

        @pl.when(even)
        def _():
            side_out[b] = before[h] + total[h]

        @pl.when(odd)
        def _():
            side_out[b] = before[h]

        @pl.when(side_sends)
        def _():
            side_copy(b).start()

    y_start(0)

    @pl.when(odd)
    def _():
        for o in range(CORES):
            swap_query(o, c).start()

    send_late(-1)
    held_early = [SWAP] + [first_late + b for b in range(LATE)]
    q_start(0)
    for t in range(3):
        chip_start(0, t)
    for h in held_early:
        for t in range(2):
            chip_start(h, t)
    for g in range(1, AHEAD):
        y_start(g)

    @pl.when(even)
    def _():
        for b in range(LATE):
            @pl.when(here(first_late + b))
            def _():
                q_start(first_late + b)

    q_start(1)
    for t in range(3):
        chip_start(1, t)
    for h in held_early:
        for t in range(2):
            chip_wait(h, t)

    for h in [SWAP] + [first_early + b for b in range(EARLY)]:
        total[h] = dot_tn(kb[h], vb[h])

    @pl.when(even)
    def _():
        side_out[EARLY] = total[SWAP]
        side_copy(EARLY).start()

    def step(h, _):
        slot = lax.rem(h, NEXT)
        is_early = h >= first_early
        chain_due = both(h >= LAG, h < first_early + LAG)

        def needs(g):
            return both(g < first_late, g != SWAP)

        for t in range(2):
            @pl.when(needs(h + 2))
            def _():
                chip_start(h + 2, t)

            @pl.when(needs(h))
            def _():
                chip_wait(h, t)

        @pl.when(h + 2 < heads)
        def _():
            chip_start(h + 2, 2)

        late_next = late_heads(level + 1)
        @pl.when(both(chain_due, level == 2))
        def _():
            chain(h - LAG)

        chip_wait(h, 2)
        own_part(h, slot)

        @pl.when(h == lax.rem(level, heads))
        def _():
            for b in range(EARLY):
                chain_early(b)

        send_late(h)

        extra = both(even, has_after, h < late_next)
        usual = jnp.logical_or(ahead(h), local(h))

        def serve_next(j, _):
            g = jnp.where(j == 0, heads - late_next + h, h)
            alone = local(g)

            @pl.when(jnp.logical_not(alone))
            def _():
                for s in range(CORES):
                    q_copy(g, c, s).wait_recv()

            next_part(
                jnp.where(alone, 0, 1), g,
                jnp.where(alone, 2 * heads + g - first_late, g),
            )

            @pl.when(jnp.logical_not(serves(g)))
            def _():
                serve(g)

            return 0

        lax.fori_loop(jnp.where(extra, 0, 1), jnp.where(usual, 2, 1), serve_next, 0)

        @pl.when(both(chain_due, level > 2))
        def _():
            chain(h - LAG)

        @pl.when(both(h + 2 < heads, jnp.logical_or(odd, jnp.logical_not(here(h + 2)))))
        def _():
            q_start(h + 2)

        def prepare(g, at):
            @pl.when(has_before)
            def _():
                merge_back(g, at)

            add_state(g, at)

        @pl.when(h >= LAG)
        def _():
            g = h - LAG
            at = lax.rem(g, NEXT)

            @pl.when(both(odd, g == SWAP))
            def _():
                swap_copy(0).wait_recv()
                swap_copy(1).wait_recv()
                merge(CAME, heads, at)

            prepare(g, at)
            emit(g, at)

        def add_side(g):
            @pl.when(side_gets)
            def _():
                side_copy(g - first_early).wait_recv()
                before[g] += side_in[g - first_early]

        def ready(g):
            return both(g >= first_early, jnp.logical_or(level == 0, here(g)))

        @pl.when(ready(h))
        def _():
            add_side(h)
            prepare(h, slot)

        pass_late(h)

        @pl.when(crossed(h))
        def _():
            y_arrived(h)

        y_sent(h)

        @pl.when(h + AHEAD < heads)
        def _():
            y_start(h + AHEAD)

        @pl.when(both(crossed(h), jnp.logical_not(is_early)))
        def _():
            total_y[h] = dot_tn(kb[heads + h], vb[heads + h])

        @pl.when(both(level == 0, jnp.logical_not(is_early)))
        def _():
            chain(h)

        swap_now = both(even, h == SWAP_STEP)

        @pl.when(swap_now)
        def _():
            o_acc[EXTRA] = jnp.zeros((span, DH), F32)
            l_acc[EXTRA] = jnp.zeros((span, DH), F32)
            m_acc[EXTRA] = jnp.full((span, DH), NEG, F32)
            for s in range(CORES):
                swap_query(c, s).wait_recv()

        def cross(j, _):
            mine = j == 1
            ahead_now = serves(h)
            cross_part(
                jnp.where(both(mine, ahead_now), 1, 0),
                jnp.where(mine, h, heads),
                jnp.where(mine, heads + h, SWAP),
                jnp.where(mine, jnp.where(ahead_now, NEXT, slot), EXTRA),
            )
            return 0

        lax.fori_loop(jnp.where(swap_now, 0, 1), jnp.where(crossed(h), 2, 1), cross, 0)

        @pl.when(both(level == 1, jnp.logical_not(is_early)))
        def _():
            chain(h)

        @pl.when(serves(h))
        def _():
            serve(h)

        @pl.when(swap_now)
        def _():
            pack(EXTRA, heads)
            swap_copy(0).start()
            swap_copy(1).start()

        @pl.when(ready(h))
        def _():
            emit(h, slot)

        @pl.when(h == heads - 1)
        def _():
            for b in range(EARLY):
                g = first_early + b

                @pl.when(jnp.logical_not(ready(g)))
                def _():
                    add_side(g)
                    prepare(g, g % NEXT)
                    emit(g, g % NEXT)

        return 0

    lax.fori_loop(0, heads, step, 0)

    def drain(h, _):
        for t in range(3):
            mate_copy(h, t).wait_send()
        out_mate(h).wait_send()
        out_mate(h).wait_recv()
        out_own(h).wait()

        @pl.when(gives(h))
        def _():
            served_copy(h, 0).wait_send()
            served_copy(h, 1).wait_send()

        @pl.when(has_after)
        def _():
            state_copy(h).wait_send()

        @pl.when(takes(h))
        def _():
            for o in range(CORES):
                q_copy(h, o, c).wait_send()

        return 0

    lax.fori_loop(0, heads, drain, 0)

    @pl.when(side_sends)
    def _():
        for b in range(EARLY):
            side_copy(b).wait_send()

    @pl.when(even)
    def _():
        side_copy(EARLY).wait_send()
        for t in range(2):
            swap_copy(t).wait_send()

    @pl.when(odd)
    def _():
        for o in range(CORES):
            swap_query(o, c).wait_send()

    for b in range(LATE):
        h = first_late + b

        @pl.when(both(odd, here(h)))
        def _():
            for t in range(2):
                for s in range(CORES):
                    y_pass(h, s, t).wait_send()

        @pl.when(both(odd, has_after, jnp.logical_not(ahead(h))))
        def _():
            for t in range(2):
                for o in range(CORES):
                    f_copy(b, o, t, c).wait_send()


def per_device(query_rows, key_rows, value_rows):
    rows = query_rows.shape[0]
    layer = WINDOW // rows
    assert layer == 2 * CORES
    levels = lax.axis_size("seq") // layer
    heads = H // CORES
    span = CORES * rows
    dma = pltpu.SemaphoreType.DMA
    return pl.pallas_call(
        functools.partial(kernel, levels, rows),
        out_shape=jax.ShapeDtypeStruct(query_rows.shape, BF16),
        in_specs=[pl.BlockSpec(memory_space=pl.ANY)] * 3,
        out_specs=pl.BlockSpec(memory_space=pl.ANY),
        scratch_shapes=[pltpu.VMEM((2, heads + 1, span, DH), BF16)]
        + [pltpu.VMEM((2 * heads + LATE, span, DH), BF16)] * 2
        + [pltpu.VMEM((heads, span, DH), BF16)]
        + [pltpu.VMEM((2, heads + 1, span, DH), BF16)]
        + [pltpu.VMEM((2, heads + 1, 1, span), F32)]
        + [pltpu.VMEM((EXTRA + 1, span, DH), F32)] * 3
        + [pltpu.VMEM((NEXT, span, DH), F32)]
        + [pltpu.VMEM((heads, DH, DH), F32)] * 5
        + [pltpu.VMEM((EARLY + 1, DH, DH), F32)] * 2
        + [
            dma((heads, 3)),
            dma((heads, 3)),
            dma((heads, 3)),
            dma((heads, CORES, 2)),
            dma((heads, CORES, 2)),
            dma((LATE, CORES, 2)),
            dma((LATE, CORES, 2)),
            dma((heads, CORES)),
            dma((heads, CORES)),
            dma((heads,)),
            dma((heads,)),
            dma((EARLY + 1,)),
            dma((EARLY + 1,)),
            dma((heads, 2)),
            dma((heads, 2)),
            dma((heads,)),
            dma((heads,)),
            dma((heads,)),
            dma((CORES,)),
            dma((CORES,)),
            dma((2,)),
            dma((2,)),
        ],
        compiler_params=pltpu.CompilerParams(
            collective_id=0, has_side_effects=True, vmem_limit_bytes=56 * 2**20
        ),
    )(query_rows, key_rows, value_rows)


def solution(mesh):
    spec = P(("group", "seq"), None)
    return jax.shard_map(
        per_device, mesh=mesh, in_specs=(spec, spec, spec), out_specs=spec, check_vma=False
    )
```

```python
import functools
import math

import jax
import jax.numpy as jnp
from jax import lax
from jax.experimental import pallas as pl
from jax.experimental.pallas import tpu as pltpu
from jax.sharding import PartitionSpec as P

H = 16
DH = 128
WINDOW = 2048
TILE = 256
CORES = 2
LATE = 3
EARLY = 2
SWAP = 4
SWAP_STEP = 2
SEND_AT = (-1, -1, -1, -1, -1, -1)
LAG = 2
NEXT = LAG + 1
EXTRA = NEXT + 1
SENT, CAME = 0, 1
AHEAD = 3
EPSILON = 1e-06
EXP_SCALE = math.log2(math.e) / math.sqrt(DH)
NEG = -1e30
F32 = jnp.float32
BF16 = jnp.bfloat16
MESH = pl.DeviceIdType.MESH


def dot_nt(a, b):
    return lax.dot_general(a, b, (((1,), (1,)), ((), ())), preferred_element_type=F32)


def dot_tn(a, b):
    return lax.dot_general(a, b, (((0,), (0,)), ((), ())), preferred_element_type=F32)


def dot_nn(a, b):
    return jnp.dot(a, b, preferred_element_type=F32)


def times_state(q, state):
    high = state.astype(BF16)
    low = (state - high.astype(F32)).astype(BF16)
    both = dot_nn(q, jnp.concatenate([high, low], axis=1))
    return both[:, :DH] + both[:, DH:]


def head_norm(x):
    return x * lax.rsqrt(jnp.mean(x * x, axis=-1, keepdims=True) + EPSILON)


def late_heads(level):
    return jnp.minimum(level, LATE)


def kernel(
    levels, rows,
    q_hbm, k_hbm, v_hbm, out_hbm,
    qb, kb, vb, ob, o_part, w_part,
    o_acc, m_acc, l_acc, lin_acc, total, total_y, before, state_in, state_out, side_in, side_out,
    own_sem, m_send, m_recv, y_send, y_recv, f_send, f_recv, q_send, q_recv,
    s_send, s_recv, e_send, e_recv, b_send, b_recv, o_own, o_send, o_recv, x_send, x_recv, g_send, g_recv,
):
    me = lax.axis_index("seq")
    c = lax.rem(me, CORES)
    side = lax.rem(me // CORES, 2)
    level = me // (2 * CORES)
    heads = H // CORES
    first_late = heads - LATE
    first_early = heads - EARLY
    span = CORES * rows
    tiles = span // TILE
    even = side == 0
    odd = side == 1
    has_before = level > 0
    has_after = level < levels - 1

    def both(*conds):
        out = conds[0]
        for x in conds[1:]:
            out = jnp.logical_and(out, x)
        return out

    def device(dz, ds, core):
        s = side if ds == 0 else 1 - side
        return {"seq": ((level + dz) * 2 + s) * CORES + core}

    mate = device(0, 0, 1 - c)

    def ahead(h):
        return both(has_after, h < heads - late_heads(level + 1))

    def here(h):
        return both(has_before, h >= heads - late_heads(level))

    def local(h):
        return both(odd, here(h))

    def gives(h):
        return both(has_after, jnp.logical_or(even, ahead(h)))

    def takes(h):
        return both(has_before, jnp.logical_not(local(h)))

    def crossed(h):
        return jnp.logical_or(
            both(odd, h != SWAP), both(even, jnp.logical_or(ahead(h), here(h)))
        )

    def serves(h):
        return both(even, ahead(h))

    barrier = pltpu.get_barrier_semaphore()

    def greet(dev):
        pl.semaphore_signal(barrier, inc=1, device_id=dev, device_id_type=MESH)

    greet(mate)
    for o in range(CORES):
        greet(device(0, 1, o))

    @pl.when(has_before)
    def _():
        for o in range(CORES):
            greet(device(-1, 0, o))

    @pl.when(has_after)
    def _():
        for o in range(CORES):
            greet(device(1, 0, o))

    ends = has_before.astype(jnp.int32) + has_after.astype(jnp.int32)
    pl.semaphore_wait(barrier, 1 + CORES + CORES * ends)

    kv_hbm = (k_hbm, v_hbm)
    sources = (k_hbm, v_hbm, q_hbm)

    def columns(owner, h):
        return pl.ds(pl.multiple_of((owner * heads + h) * DH, DH), DH)

    def part(core):
        return pl.ds(pl.multiple_of(core * rows, rows), rows)

    def chip_target(t, h):
        return (kb, vb)[t].at[h, part(c), :] if t < 2 else qb.at[0, h, part(c), :]

    def own_copy(h, t):
        return pltpu.make_async_copy(
            sources[t].at[:, columns(c, h)], chip_target(t, h), own_sem.at[h, t]
        )

    def remote(src, dst, send, recv, dev):
        return pltpu.make_async_remote_copy(
            src_ref=src, dst_ref=dst, send_sem=send, recv_sem=recv,
            device_id=dev, device_id_type=MESH,
        )

    def mate_copy(h, t):
        return remote(
            sources[t].at[:, columns(1 - c, h)], chip_target(t, h),
            m_send.at[h, t], m_recv.at[h, t], mate,
        )

    def y_copy(h, o, t):
        return remote(
            kv_hbm[t].at[:, columns(o, h)], (kb, vb)[t].at[heads + h, part(c), :],
            y_send.at[h, o, t], y_recv.at[h, c, t], device(0, 1, o),
        )

    def y_pass(h, s, t):
        b = h - first_late
        return remote(
            (kb, vb)[t].at[2 * heads + b, part(s), :], (kb, vb)[t].at[heads + h, part(s), :],
            y_send.at[h, s, t], y_recv.at[h, s, t], device(0, 1, c),
        )

    def f_copy(b, o, t, s):
        h = first_late + b
        return remote(
            kv_hbm[t].at[:, columns(o, h)], (kb, vb)[t].at[2 * heads + b, part(s), :],
            f_send.at[b, o, t], f_recv.at[b, s, t], device(1, 0, o),
        )

    def q_copy(h, o, s):
        return remote(
            q_hbm.at[:, columns(o, h)], qb.at[1, h, part(s), :],
            q_send.at[h, o], q_recv.at[h, s], device(-1, 0, o),
        )

    def served_copy(h, t):
        return remote(
            (o_part, w_part)[t].at[SENT, h], (o_part, w_part)[t].at[CAME, h],
            b_send.at[h, t], b_recv.at[h, t], device(1, 0, c),
        )

    def state_copy(h):
        return remote(
            state_out.at[h], state_in.at[h], s_send.at[h], s_recv.at[h], device(1, 0, c)
        )

    def swap_query(o, s):
        return remote(
            q_hbm.at[:, columns(o, SWAP)], qb.at[0, heads, part(s), :],
            x_send.at[o], x_recv.at[s], device(0, 1, o),
        )

    def swap_copy(t):
        return remote(
            (o_part, w_part)[t].at[SENT, heads], (o_part, w_part)[t].at[CAME, heads],
            g_send.at[t], g_recv.at[t], device(0, 1, c),
        )

    def side_copy(b):
        return remote(
            side_out.at[b], side_in.at[b], e_send.at[b], e_recv.at[b], device(0, 1, c)
        )

    def out_own(h):
        return pltpu.make_async_copy(
            ob.at[h, part(c), :], out_hbm.at[:, columns(c, h)], o_own.at[h]
        )

    def out_mate(h):
        return remote(
            ob.at[h, part(1 - c), :], out_hbm.at[:, columns(c, h)],
            o_send.at[h], o_recv.at[h], mate,
        )

    def chip_start(h, t):
        own_copy(h, t).start()
        mate_copy(h, t).start()

    def chip_wait(h, t):
        own_copy(h, t).wait()
        mate_copy(h, t).wait_recv()

    def direct(h):
        return jnp.logical_or(both(even, h != SWAP), both(odd, ahead(h)))

    def y_start(h):
        @pl.when(direct(h))
        def _():
            for t in range(2):
                for o in range(CORES):
                    y_copy(h, o, t).start()

    def y_sent(h):
        @pl.when(direct(h))
        def _():
            for t in range(2):
                for o in range(CORES):
                    y_copy(h, o, t).wait_send()

    def pass_late(step):
        for b in range(LATE):
            h = first_late + b
            at = h - 3

            @pl.when(both(odd, here(h), step == at))
            def _():
                for t in range(2):
                    for s in range(CORES):
                        f_copy(b, c, t, s).wait_recv()
                        y_pass(h, s, t).start()

    def y_arrived(h):
        for t in range(2):
            for s in range(CORES):
                y_pass(h, s, t).wait_recv()

    def q_start(h):
        @pl.when(takes(h))
        def _():
            for o in range(CORES):
                q_copy(h, o, c).start()

    def send_late(step):
        count = late_heads(level + 1)
        for chunk, at in enumerate(SEND_AT):
            @pl.when(both(odd, has_after, chunk < 2 * count, step == at))
            def _():
                for o in range(CORES):
                    f_copy(LATE - count + chunk // 2, o, chunk % 2, c).start()

    row_id = lax.broadcasted_iota(jnp.int32, (TILE, TILE), 0)
    col_id = lax.broadcasted_iota(jnp.int32, (TILE, TILE), 1)
    causal = row_id >= col_id
    later = col_id > row_id

    def tile(i):
        return slice(i * TILE, (i + 1) * TILE)

    def keep_part(slot, i, q, k_full, v_full, s_diag, v_diag):
        peak = jnp.max(s_diag, axis=-1, keepdims=True)
        if k_full is not None:
            s_full = dot_nt(q, k_full)
            peak = jnp.maximum(peak, jnp.max(s_full, axis=-1, keepdims=True))
        p_diag = jnp.exp2((s_diag - peak) * EXP_SCALE)
        mass = jnp.sum(p_diag, axis=-1, keepdims=True)
        acc = dot_nn(p_diag.astype(BF16), v_diag)
        if k_full is not None:
            p_full = jnp.exp2((s_full - peak) * EXP_SCALE)
            mass = mass + jnp.sum(p_full, axis=-1, keepdims=True)
            acc = acc + dot_nn(p_full.astype(BF16), v_full)
        o_acc[slot, tile(i), :] = acc
        m_acc[slot, tile(i), :] = jnp.broadcast_to(peak, (TILE, DH))
        l_acc[slot, tile(i), :] = jnp.broadcast_to(mass, (TILE, DH))

    def own_part(h, slot):
        state = jnp.zeros((DH, DH), F32)
        for i in range(tiles):
            q, k, v = qb[0, h, tile(i), :], kb[h, tile(i), :], vb[h, tile(i), :]
            scores = dot_nt(q, k)
            lin = dot_nn(jnp.where(causal, scores, 0.0).astype(BF16), v)
            if i > 0:
                lin = lin + times_state(q, state)
            lin_acc[slot, tile(i), :] = lin
            state = state + dot_tn(k, v)
            k_full = kb[h, : i * TILE, :] if i > 0 else None
            v_full = vb[h, : i * TILE, :] if i > 0 else None
            keep_part(slot, i, q, k_full, v_full, jnp.where(causal, scores, NEG), v)
        total[h] = state

    def next_part(which, h, held):
        for i in range(tiles):
            q, k, v = qb[which, h, tile(i), :], kb[held, tile(i), :], vb[held, tile(i), :]
            scores = jnp.where(later, dot_nt(q, k), NEG)
            k_full = kb[held, (i + 1) * TILE :, :] if i < tiles - 1 else None
            v_full = vb[held, (i + 1) * TILE :, :] if i < tiles - 1 else None
            keep_part(NEXT, i, q, k_full, v_full, scores, v)

    def cross_part(which, h, held, slot):
        for i in range(tiles):
            s = dot_nt(qb[which, h, tile(i), :], kb[held])
            old = m_acc[slot, tile(i), :]
            peak = jnp.maximum(old, jnp.max(s, axis=-1, keepdims=True))
            keep = jnp.exp2((old - peak) * EXP_SCALE)
            p = jnp.exp2((s - peak[:, :1]) * EXP_SCALE)
            l_acc[slot, tile(i), :] = l_acc[slot, tile(i), :] * keep + jnp.sum(
                p, axis=-1, keepdims=True
            )
            o_acc[slot, tile(i), :] = o_acc[slot, tile(i), :] * keep + dot_nn(
                p.astype(BF16), vb[held]
            )
            m_acc[slot, tile(i), :] = peak

    def pack(slot, to):
        for i in range(tiles):
            mass = l_acc[slot, tile(i), :]
            o_part[SENT, to, tile(i), :] = (o_acc[slot, tile(i), :] / mass).astype(BF16)
            weight = m_acc[slot, tile(i), :] * EXP_SCALE + jnp.log2(mass)
            w_part[SENT, to, :, tile(i)] = weight.T[:1, :]

    def serve(h):
        pack(NEXT, h)

        @pl.when(gives(h))
        def _():
            served_copy(h, 0).start()
            served_copy(h, 1).start()

    def merge_back(h, slot):
        @pl.when(takes(h))
        def _():
            served_copy(h, 0).wait_recv()
            served_copy(h, 1).wait_recv()

        merge(jnp.where(local(h), SENT, CAME), h, slot)

    def merge(src, h, slot):
        for i in range(tiles):
            weight = jnp.broadcast_to(w_part[src, h, :, tile(i)], (DH, TILE)).T
            old = m_acc[slot, tile(i), :]
            peak = jnp.maximum(old, weight * (1.0 / EXP_SCALE))
            keep = jnp.exp2((old - peak) * EXP_SCALE)
            take = jnp.exp2(weight - peak * EXP_SCALE)
            mean = o_part[src, h, tile(i), :].astype(F32)
            o_acc[slot, tile(i), :] = o_acc[slot, tile(i), :] * keep + mean * take
            l_acc[slot, tile(i), :] = l_acc[slot, tile(i), :] * keep + take
            m_acc[slot, tile(i), :] = peak

    def add_state(h, slot):
        state = before[h]
        for i in range(tiles):
            lin = lin_acc[slot, tile(i), :] + times_state(qb[0, h, tile(i), :], state)
            lin_acc[slot, tile(i), :] = head_norm(lin)

    def emit(h, slot):
        for i in range(tiles):
            win = o_acc[slot, tile(i), :] / l_acc[slot, tile(i), :]
            ob[h, tile(i), :] = (lin_acc[slot, tile(i), :] + head_norm(win)).astype(BF16)
        out_mate(h).start()
        out_own(h).start()

    def chain(h):
        @pl.when(has_before)
        def _():
            state_copy(h).wait_recv()
            before[h] = state_in[h]

        @pl.when(level == 0)
        def _():
            before[h] = jnp.zeros((DH, DH), F32)

        @pl.when(both(odd, h == SWAP))
        def _():
            side_copy(EARLY).wait_recv()
            total_y[h] = side_in[EARLY]

        @pl.when(jnp.logical_or(odd, here(h)))
        def _():
            before[h] += total_y[h]

        @pl.when(has_after)
        def _():
            state_out[h] = before[h] + total[h]

            @pl.when(serves(h))
            def _():
                state_out[h] += total_y[h]

            state_copy(h).start()

    side_sends = jnp.logical_or(even, has_before)
    side_gets = jnp.logical_or(odd, has_before)

    def chain_early(b):
        h = first_early + b

        @pl.when(has_before)
        def _():
            state_copy(h).wait_recv()
            before[h] = state_in[h]

        @pl.when(level == 0)
        def _():
            before[h] = jnp.zeros((DH, DH), F32)

        @pl.when(has_after)
        def _():
            state_out[h] = before[h] + total[h]
            state_copy(h).start()

        @pl.when(even)
        def _():
            side_out[b] = before[h] + total[h]

        @pl.when(odd)
        def _():
            side_out[b] = before[h]

        @pl.when(side_sends)
        def _():
            side_copy(b).start()

    y_start(0)

    @pl.when(odd)
    def _():
        for o in range(CORES):
            swap_query(o, c).start()

    send_late(-1)
    held_early = [SWAP] + [first_late + b for b in range(LATE)]
    q_start(0)
    for t in range(3):
        chip_start(0, t)
    for h in held_early:
        for t in range(2):
            chip_start(h, t)
    for g in range(1, AHEAD):
        y_start(g)

    @pl.when(even)
    def _():
        for b in range(LATE):
            @pl.when(here(first_late + b))
            def _():
                q_start(first_late + b)

    q_start(1)
    for t in range(3):
        chip_start(1, t)
    for h in held_early:
        for t in range(2):
            chip_wait(h, t)

    for h in [SWAP] + [first_early + b for b in range(EARLY)]:
        total[h] = dot_tn(kb[h], vb[h])

    @pl.when(even)
    def _():
        side_out[EARLY] = total[SWAP]
        side_copy(EARLY).start()

    def step(h, _):
        slot = lax.rem(h, NEXT)
        is_early = h >= first_early
        chain_due = both(h >= LAG, h < first_early + LAG)

        def needs(g):
            return both(g < first_late, g != SWAP)

        for t in range(2):
            @pl.when(needs(h + 2))
            def _():
                chip_start(h + 2, t)

            @pl.when(needs(h))
            def _():
                chip_wait(h, t)

        @pl.when(h + 2 < heads)
        def _():
            chip_start(h + 2, 2)

        late_next = late_heads(level + 1)
        @pl.when(both(chain_due, level == 2))
        def _():
            chain(h - LAG)

        chip_wait(h, 2)
        own_part(h, slot)

        @pl.when(h == lax.rem(level, heads))
        def _():
            for b in range(EARLY):
                chain_early(b)

        send_late(h)

        extra = both(even, has_after, h < late_next)
        usual = jnp.logical_or(ahead(h), local(h))

        def serve_next(j, _):
            g = jnp.where(j == 0, heads - late_next + h, h)
            alone = local(g)

            @pl.when(jnp.logical_not(alone))
            def _():
                for s in range(CORES):
                    q_copy(g, c, s).wait_recv()

            next_part(
                jnp.where(alone, 0, 1), g,
                jnp.where(alone, 2 * heads + g - first_late, g),
            )

            @pl.when(jnp.logical_not(serves(g)))
            def _():
                serve(g)

            return 0

        lax.fori_loop(jnp.where(extra, 0, 1), jnp.where(usual, 2, 1), serve_next, 0)

        @pl.when(both(chain_due, level > 2))
        def _():
            chain(h - LAG)

        @pl.when(both(h + 2 < heads, jnp.logical_or(odd, jnp.logical_not(here(h + 2)))))
        def _():
            q_start(h + 2)

        def prepare(g, at):
            @pl.when(has_before)
            def _():
                merge_back(g, at)

            add_state(g, at)

        @pl.when(h >= LAG)
        def _():
            g = h - LAG
            at = lax.rem(g, NEXT)

            @pl.when(both(odd, g == SWAP))
            def _():
                swap_copy(0).wait_recv()
                swap_copy(1).wait_recv()
                merge(CAME, heads, at)

            prepare(g, at)
            emit(g, at)

        def add_side(g):
            @pl.when(side_gets)
            def _():
                side_copy(g - first_early).wait_recv()
                before[g] += side_in[g - first_early]

        def ready(g):
            return both(g >= first_early, jnp.logical_or(level == 0, here(g)))

        def finish_late(g):
            @pl.when(jnp.logical_not(ready(g)))
            def _():
                add_side(g)
                prepare(g, g % NEXT)
                emit(g, g % NEXT)

        @pl.when(both(odd, h == heads - 1))
        def _():
            for b in range(EARLY - 1):
                finish_late(first_early + b)

        @pl.when(ready(h))
        def _():
            add_side(h)
            prepare(h, slot)

        pass_late(h)

        @pl.when(crossed(h))
        def _():
            y_arrived(h)

        y_sent(h)

        @pl.when(h + AHEAD < heads)
        def _():
            y_start(h + AHEAD)

        @pl.when(both(crossed(h), jnp.logical_not(is_early)))
        def _():
            total_y[h] = dot_tn(kb[heads + h], vb[heads + h])

        @pl.when(both(level == 0, jnp.logical_not(is_early)))
        def _():
            chain(h)

        swap_now = both(even, h == SWAP_STEP)

        @pl.when(swap_now)
        def _():
            o_acc[EXTRA] = jnp.zeros((span, DH), F32)
            l_acc[EXTRA] = jnp.zeros((span, DH), F32)
            m_acc[EXTRA] = jnp.full((span, DH), NEG, F32)
            for s in range(CORES):
                swap_query(c, s).wait_recv()

        def cross(j, _):
            mine = j == 1
            ahead_now = serves(h)
            cross_part(
                jnp.where(both(mine, ahead_now), 1, 0),
                jnp.where(mine, h, heads),
                jnp.where(mine, heads + h, SWAP),
                jnp.where(mine, jnp.where(ahead_now, NEXT, slot), EXTRA),
            )
            return 0

        lax.fori_loop(jnp.where(swap_now, 0, 1), jnp.where(crossed(h), 2, 1), cross, 0)

        @pl.when(both(level == 1, jnp.logical_not(is_early)))
        def _():
            chain(h)

        @pl.when(serves(h))
        def _():
            serve(h)

        @pl.when(swap_now)
        def _():
            pack(EXTRA, heads)
            swap_copy(0).start()
            swap_copy(1).start()

        @pl.when(ready(h))
        def _():
            emit(h, slot)

        @pl.when(h == heads - 1)
        def _():
            @pl.when(even)
            def _():
                for b in range(EARLY - 1):
                    finish_late(first_early + b)

            finish_late(heads - 1)

        return 0

    lax.fori_loop(0, heads, step, 0)

    def drain(h, _):
        for t in range(3):
            mate_copy(h, t).wait_send()
        out_mate(h).wait_send()
        out_mate(h).wait_recv()
        out_own(h).wait()

        @pl.when(gives(h))
        def _():
            served_copy(h, 0).wait_send()
            served_copy(h, 1).wait_send()

        @pl.when(has_after)
        def _():
            state_copy(h).wait_send()

        @pl.when(takes(h))
        def _():
            for o in range(CORES):
                q_copy(h, o, c).wait_send()

        return 0

    lax.fori_loop(0, heads, drain, 0)

    @pl.when(side_sends)
    def _():
        for b in range(EARLY):
            side_copy(b).wait_send()

    @pl.when(even)
    def _():
        side_copy(EARLY).wait_send()
        for t in range(2):
            swap_copy(t).wait_send()

    @pl.when(odd)
    def _():
        for o in range(CORES):
            swap_query(o, c).wait_send()

    for b in range(LATE):
        h = first_late + b

        @pl.when(both(odd, here(h)))
        def _():
            for t in range(2):
                for s in range(CORES):
                    y_pass(h, s, t).wait_send()

        @pl.when(both(odd, has_after, jnp.logical_not(ahead(h))))
        def _():
            for t in range(2):
                for o in range(CORES):
                    f_copy(b, o, t, c).wait_send()


def per_device(query_rows, key_rows, value_rows):
    rows = query_rows.shape[0]
    layer = WINDOW // rows
    assert layer == 2 * CORES
    levels = lax.axis_size("seq") // layer
    heads = H // CORES
    span = CORES * rows
    dma = pltpu.SemaphoreType.DMA
    return pl.pallas_call(
        functools.partial(kernel, levels, rows),
        out_shape=jax.ShapeDtypeStruct(query_rows.shape, BF16),
        in_specs=[pl.BlockSpec(memory_space=pl.ANY)] * 3,
        out_specs=pl.BlockSpec(memory_space=pl.ANY),
        scratch_shapes=[pltpu.VMEM((2, heads + 1, span, DH), BF16)]
        + [pltpu.VMEM((2 * heads + LATE, span, DH), BF16)] * 2
        + [pltpu.VMEM((heads, span, DH), BF16)]
        + [pltpu.VMEM((2, heads + 1, span, DH), BF16)]
        + [pltpu.VMEM((2, heads + 1, 1, span), F32)]
        + [pltpu.VMEM((EXTRA + 1, span, DH), F32)] * 3
        + [pltpu.VMEM((NEXT, span, DH), F32)]
        + [pltpu.VMEM((heads, DH, DH), F32)] * 5
        + [pltpu.VMEM((EARLY + 1, DH, DH), F32)] * 2
        + [
            dma((heads, 3)),
            dma((heads, 3)),
            dma((heads, 3)),
            dma((heads, CORES, 2)),
            dma((heads, CORES, 2)),
            dma((LATE, CORES, 2)),
            dma((LATE, CORES, 2)),
            dma((heads, CORES)),
            dma((heads, CORES)),
            dma((heads,)),
            dma((heads,)),
            dma((EARLY + 1,)),
            dma((EARLY + 1,)),
            dma((heads, 2)),
            dma((heads, 2)),
            dma((heads,)),
            dma((heads,)),
            dma((heads,)),
            dma((CORES,)),
            dma((CORES,)),
            dma((2,)),
            dma((2,)),
        ],
        compiler_params=pltpu.CompilerParams(
            collective_id=0, has_side_effects=True, vmem_limit_bytes=56 * 2**20
        ),
    )(query_rows, key_rows, value_rows)


def solution(mesh):
    spec = P(("group", "seq"), None)
    return jax.shard_map(
        per_device, mesh=mesh, in_specs=(spec, spec, spec), out_specs=spec, check_vma=False
    )
```
